128 devices in a mesh: walk: 16 (over x, z), pan: 8 (over y, core).
Axes of the slice: x: 4, y: 4, z: 4, core: 2. Of those that a mesh axis runs over, the one named last changes fastest.
Arguments:
- dlog: bfloat16 [32768, 4096], P('walk', 'pan'), may hold values from 0 to 2
- dener: bfloat16 [32768, 4096], P('walk', 'pan'), may hold values from -0.5 to 2.5
- energy: float32 [32768], P('walk'), may hold values from -3 to -1
- mask: int32 [16], replicated, may hold values 0 or 1
- owner: int32 [16], replicated, may hold values from 0 to 15, each once
Outputs:
- correlation: float32 [4096, 4096], P('walk', 'pan')
- hamilton: float32 [4096, 4096], P('walk', 'pan')
The draws below stay inside these ranges and needn't reach their ends.
Inputs may be any that keep to these rules, and one draw needn't show every extreme that they name: `owner`: each block number appears once.
All inputs are finite; a program needn't handle non-finite values.
Results may differ from the reference program's by a relative error of at most 0.005.
Values may be sent and summed in bfloat16 or wider, within the bound.
A program may use at most 128 MiB of HBM per device.

```python
import jax
import jax.numpy as jnp
from jax import lax

P_SIZE = 4096
BLOCK = 256
W = 32768
NB = 16


def set_ends(drawn, rng, least, top_value):
    extent = drawn.shape
    spot = [jax.random.randint(jax.random.fold_in(rng, axis), (), 0, extent[axis]) for axis in range(len(extent))]
    drawn = drawn.at[tuple(spot)].set(least)
    longest = extent.index(max(extent))
    spot[longest] = (spot[longest] + 1) % extent[longest]
    return drawn.at[tuple(spot)].set(top_value)


def block_scale(rng, extent, cuts, smallest, largest):
    factor_of, own = 1.0, jax.random.fold_in(rng, 6)
    for position, blocks in cuts:
        heights = jnp.exp(jax.random.uniform(jax.random.fold_in(own, position), (blocks,), jnp.float32, smallest / len(cuts), largest / len(cuts)))
        factor_of = factor_of * jnp.repeat(heights, extent[position] // blocks).reshape([-1 if axis == position else 1 for axis in range(len(extent))])
    return factor_of


def setup_inputs(seed: int = 0) -> dict:
    splits = jax.random.split(jax.random.key(seed), 6)
    dlog = jnp.clip(2.0 * jax.random.uniform(splits[0], (W, P_SIZE), jnp.float32) ** block_scale(splits[0], (W, P_SIZE), ((0, 16), (1, 8)), -0.2, 0.2), 0.0, 2.0).astype(jnp.bfloat16)
    dener = jnp.clip(-0.5 + 3.0 * jax.random.uniform(splits[1], (W, P_SIZE), jnp.float32) ** block_scale(splits[1], (W, P_SIZE), ((0, 16), (1, 8)), -0.2, 0.2), -0.5, 2.5).astype(jnp.bfloat16)
    energy = jnp.clip(-3.0 + 2.0 * jax.random.uniform(splits[2], (W,), jnp.float32) ** block_scale(splits[2], (W,), ((0, 16),), -0.2, 0.2), -3.0, -1.0)
    mask = set_ends((jax.random.randint(splits[3], (NB,), 0, 4) < 3).astype(jnp.int32), jax.random.fold_in(splits[3], 1), 0, 1)
    owner = jax.random.permutation(splits[4], NB).astype(jnp.int32)
    return dict(dlog=dlog, dener=dener, energy=energy, mask=mask, owner=owner)


def reference(dlog, dener, energy, mask, owner):
    total = dlog.shape[0]
    colmask = jnp.repeat(mask, BLOCK).astype(jnp.float32)
    om = dlog.astype(jnp.float32) * colmask
    gm = dener.astype(jnp.float32) * colmask
    obar = jnp.sum(om, 0) / total
    gbar = jnp.sum(gm, 0) / total
    ebar = jnp.sum(energy) / total
    ocf = om - obar
    oc = ocf.astype(jnp.bfloat16)
    hc = ((energy - ebar)[:, None] * ocf + gm - gbar).astype(jnp.bfloat16)
    ocp = jnp.take(oc.reshape(total, NB, BLOCK), owner, axis=1).reshape(total, P_SIZE)
    dims = (((0,), (0,)), ((), ()))
    correlation = lax.dot_general(ocp, oc, dims, preferred_element_type=jnp.float32) / total
    hamilton = lax.dot_general(ocp, hc, dims, preferred_element_type=jnp.float32) / total
    return correlation, hamilton
```

```python
import jax
import jax.numpy as jnp
from jax import lax
from jax.experimental import pallas as pl
from jax.experimental.pallas import tpu as pltpu
from jax.sharding import PartitionSpec as P

BLOCK = 256
ROUNDS = 4
MESH = pl.DeviceIdType.MESH
F32 = jnp.float32
BF16 = jnp.bfloat16


def wrap4(v):
    return lax.rem(v, 4)


def kernel(
    mask, owner, dlog, dener, energy, out_c, out_h,
    blocks, gown, opar, gpar, right, left_t, spread,
    part, ring1, half, ring2, whole, give, staged, stats, means, pmeans,
    local_sem, ag_send, ag_recv, pt_send, pt_recv, st_send, st_recv, mm_send, mm_recv,
    r1_send, r1_recv, r2_send, r2_recv, z_send, z_recv, f_send, f_recv,
):
    walkers = dlog.shape[0]
    total = walkers * 16
    scale = 1.0 / total
    chunk = 256
    steps = walkers // chunk

    walk = lax.axis_index("walk")
    pan = lax.axis_index("pan")
    px, pz = lax.div(walk, 4), lax.rem(walk, 4)
    py, core = lax.div(pan, 2), lax.rem(pan, 2)
    partner = (walk, py * 2 + (1 - core))

    def at_y(shift):
        return (walk, wrap4(py + shift) * 2 + core)

    def remote(src, dst, send, recv, device):
        return pltpu.make_async_remote_copy(
            src_ref=src, dst_ref=dst, send_sem=send, recv_sem=recv, device_id=device, device_id_type=MESH
        )

    own = [
        pltpu.make_async_copy(dlog.at[:, pl.ds(b * BLOCK, BLOCK)], blocks.at[b], local_sem.at[b]) for b in range(2)
    ] + [pltpu.make_async_copy(dener, gown, local_sem.at[2])]
    for copy in own:
        copy.start()

    barrier = pltpu.get_barrier_semaphore()

    def greet(d, carry):
        pl.semaphore_signal(barrier, inc=1, device_id=(lax.rem(walk + d, 16), pan), device_id_type=MESH)
        return carry

    lax.fori_loop(1, 16, greet, 0)
    for d in range(1, 4):
        pl.semaphore_signal(barrier, inc=1, device_id=at_y(d), device_id_type=MESH)
    pl.semaphore_signal(barrier, inc=1, device_id=partner, device_id_type=MESH)
    pl.semaphore_wait(barrier, 19)

    def column(b):
        return dlog.at[:, pl.ds(b * BLOCK, BLOCK)]

    gather = [
        remote(column(0), blocks.at[2], ag_send.at[0], ag_recv.at[0], at_y(1)),
        remote(column(1), blocks.at[3], ag_send.at[1], ag_recv.at[1], at_y(3)),
        remote(column(1), blocks.at[4], ag_send.at[2], ag_recv.at[2], at_y(1)),
        remote(column(0), blocks.at[5], ag_send.at[3], ag_recv.at[3], at_y(3)),
        remote(blocks.at[2], blocks.at[6], ag_send.at[4], ag_recv.at[4], at_y(1)),
        remote(blocks.at[3], blocks.at[7], ag_send.at[5], ag_recv.at[5], at_y(3)),
    ]
    for copy in gather[:4]:
        copy.start()
    pair = [
        remote(dlog, opar, pt_send.at[0], pt_recv.at[0], partner),
        remote(dener, gpar, pt_send.at[1], pt_recv.at[1], partner),
    ]
    for copy in pair:
        copy.start()

    for copy in own:
        copy.wait()
    esum = jnp.sum(energy[...])
    for b in range(2):

        def add(i, carry):
            rows = pl.ds(pl.multiple_of(i * chunk, chunk), chunk)
            o = jnp.sum(blocks[b, rows, :].astype(F32), axis=0, keepdims=True)
            g = jnp.sum(gown[rows, b * BLOCK:(b + 1) * BLOCK].astype(F32), axis=0, keepdims=True)
            return carry[0] + o, carry[1] + g

        zero = jnp.zeros((1, BLOCK), F32)
        o, g = lax.fori_loop(0, steps, add, (zero, zero))
        stats[walk, b] = jnp.concatenate([o, g, jnp.full((1, BLOCK), esum, F32), jnp.zeros((5, BLOCK), F32)], axis=0)

    def stat_copy(d):
        return remote(
            stats.at[walk], stats.at[walk], st_send.at[d], st_recv.at[d], (lax.rem(walk + d, 16), pan)
        )

    def stat_start(d, carry):
        stat_copy(d).start()
        return carry

    def stat_wait(d, carry):
        stat_copy(d).wait()
        return carry

    lax.fori_loop(1, 16, stat_start, 0)
    lax.fori_loop(1, 16, stat_wait, 0)
    sums = stats[0]
    for i in range(1, 16):
        sums = sums + stats[i]
    means[py] = sums * scale
    shared = [remote(means.at[py], means.at[py], mm_send.at[d], mm_recv.at[d], at_y(d)) for d in range(1, 4)] + [
        remote(means.at[py], pmeans, mm_send.at[0], mm_recv.at[0], partner)
    ]
    for copy in shared:
        copy.start()

    ebar = means[py, 0, 2:3, 0:128]
    for i in range(walkers // 128):
        row = energy[i:i + 1, :] - ebar
        spread[i * 128:(i + 1) * 128, :] = jnp.broadcast_to(row, (128, 128)).T

    def build(o_of, g_of, obar, gbar, m, tile):
        def step(i, carry):
            rows = pl.ds(pl.multiple_of(i * chunk, chunk), chunk)
            oc = o_of(rows).astype(F32) * m - obar
            e = spread[rows, :]
            hc = jnp.concatenate([e, e], axis=1) * oc + g_of(rows).astype(F32) * m - gbar
            right[0, tile, rows, :] = oc.astype(BF16)
            right[1, tile, rows, :] = hc.astype(BF16)
            return carry

        lax.fori_loop(0, steps, step, 0)

    for b in range(2):
        m = mask[py * 4 + core * 2 + b].astype(F32)
        build(
            lambda rows, b=b: blocks[b, rows, :],
            lambda rows, b=b: gown[rows, b * BLOCK:(b + 1) * BLOCK],
            means[py, b, 0:1, :] * m,
            means[py, b, 1:2, :] * m,
            m,
            core * 2 + b,
        )
    for copy in pair:
        copy.wait()
    for copy in shared:
        copy.wait()
    for b in range(2):
        m = mask[py * 4 + (1 - core) * 2 + b].astype(F32)
        build(
            lambda rows, b=b: opar[rows, b * BLOCK:(b + 1) * BLOCK],
            lambda rows, b=b: gpar[rows, b * BLOCK:(b + 1) * BLOCK],
            pmeans[b, 0:1, :] * m,
            pmeans[b, 1:2, :] * m,
            m,
            (1 - core) * 2 + b,
        )

    xs = (px, (wrap4(px + 1) * 4 + pz, pan), (wrap4(px + 3) * 4 + pz, pan))
    zs = (pz, (px * 4 + wrap4(pz + 1), pan), (px * 4 + wrap4(pz + 3), pan))

    def ring(buf, got, send, recv, axis):
        me, up, down = axis
        far, nxt, prv = wrap4(me + 2), wrap4(me + 1), wrap4(me + 3)
        return [
            remote(buf.at[0, far], got.at[0], send.at[0], recv.at[0], up),
            remote(buf.at[1, far], got.at[1], send.at[1], recv.at[1], down),
            remote(buf.at[1, nxt], got.at[2], send.at[2], recv.at[2], up),
            remote(buf.at[0, prv], got.at[3], send.at[3], recv.at[3], down),
            remote(buf.at[0, nxt], got.at[4], send.at[4], recv.at[4], up),
            remote(buf.at[1, prv], got.at[5], send.at[5], recv.at[5], down),
        ]

    def ring1_of(r, ch):
        return ring(part.at[r, ch], ring1.at[r, ch], r1_send.at[r, ch], r1_recv.at[r, ch], (xs, zs)[ch])

    def ring2_of(r, ch):
        return ring(half.at[r, ch], ring2.at[r, ch], r2_send.at[r, ch], r2_recv.at[r, ch], (zs, xs)[ch])

    def ring_start(copies):
        for copy in copies[:4]:
            copy.start()

    def ring_mid(copies, buf, got, axis):
        me = axis[0]
        for b, shift in ((0, 1), (1, 3)):
            copies[b].wait_recv()
            k = wrap4(me + shift)
            buf[b, k] = (buf[b, k].astype(F32) + got[b].astype(F32)).astype(BF16)
            copies[4 + b].start()

    def source(r, b):
        second = lax.div(r, 2) * (3 - r)
        middle = r - second - 3 * lax.div(r, 3)
        ysrc = wrap4(py + middle * (1 if b else 3) + 2 * lax.div(r, 3))
        bsel = b + second * (1 - 2 * b)
        return ysrc, bsel

    def block_of(r, b):
        ysrc, bsel = source(r, b)
        return ysrc * 4 + core * 2 + bsel

    def give_copy(r, b):
        return remote(give.at[r, b], whole.at[block_of(r, b)], z_send.at[r, b], z_recv.at[r, b], partner)

    def one_round(r, carry):
        for t in range(1, ROUNDS):

            @pl.when(r == t)
            def _():
                for b in range(2):
                    gather[2 * (t - 1) + b].wait_recv()
                    if t == 1:
                        gather[4 + b].start()

        for b in range(2):
            ysrc, bsel = source(r, b)
            m = mask[ysrc * 4 + core * 2 + bsel].astype(F32)
            obar = means[ysrc, bsel, 0:1, :] * m

            def turn(i, c):
                rows = pl.ds(pl.multiple_of(i * chunk, chunk), chunk)
                oc = blocks[2 * r + b, rows, :].astype(F32) * m - obar
                left_t[b * BLOCK:(b + 1) * BLOCK, rows] = oc.T.astype(BF16)
                return c

            lax.fori_loop(0, steps, turn, 0)

        for ch in range(2):
            for tile in range(4):
                product = jnp.dot(left_t[...], right[ch, tile], preferred_element_type=F32)
                h, off = tile // 2, (tile % 2) * BLOCK
                part[r, ch, :, :, h, :, off:off + BLOCK] = product.astype(BF16).reshape(2, 4, 64, BLOCK)
            ring_start(ring1_of(r, ch))

        for ch in range(2):
            ring_mid(ring1_of(r, ch), part.at[r, ch], ring1.at[r, ch], (xs, zs)[ch])
        for ch in range(2):
            copies = ring1_of(r, ch)
            me = (px, pz)[ch]
            for b, (i, j) in enumerate(((3, 4), (2, 5))):
                copies[i].wait_recv()
                copies[j].wait_recv()
                for k in range(4):
                    rows = slice(16 * k, 16 * k + 16)
                    value = (
                        part[r, ch, b, me, :, rows, :].astype(F32)
                        + ring1[r, ch, i, :, rows, :].astype(F32)
                        + ring1[r, ch, j, :, rows, :].astype(F32)
                    )
                    half[r, ch, b, k] = value.astype(BF16)
            ring_start(ring2_of(r, ch))
        for ch in range(2):
            ring_mid(ring2_of(r, ch), half.at[r, ch], ring2.at[r, ch], (zs, xs)[ch])
        for b, (i, j) in enumerate(((3, 4), (2, 5))):
            for ch in range(2):
                copies = ring2_of(r, ch)
                me = (pz, px)[ch]
                copies[i].wait_recv()
                copies[j].wait_recv()

                def value(h):
                    return (
                        half[r, ch, b, me, h].astype(F32)
                        + ring2[r, ch, i, h].astype(F32)
                        + ring2[r, ch, j, h].astype(F32)
                    ) * scale

                whole[block_of(r, b), ch] = value(core)
                give[r, b, ch] = value(1 - core)
            give_copy(r, b).start()
        return carry

    lax.fori_loop(0, ROUNDS, one_round, 0)

    def give_wait(r, carry):
        for b in range(2):
            give_copy(r, b).wait()
        return carry

    lax.fori_loop(0, ROUNDS, give_wait, 0)

    row_c = pl.multiple_of(px * 64 + pz * 16, 16)
    row_h = pl.multiple_of(pz * 64 + px * 16, 16)

    def place(r, d):
        return [
            remote(
                staged.at[r, ch],
                (out_c, out_h)[ch].at[pl.ds((row_c, row_h)[ch], 16), :],
                f_send.at[d, ch],
                f_recv.at[d, ch],
                (r, pan),
            )
            for ch in range(2)
        ]

    def place_start(d, carry):
        r = lax.rem(walk + d, 16)
        staged[r] = whole[owner[r]]
        for copy in place(r, d):
            copy.start()
        return carry

    def place_wait(d, carry):
        for copy in place(lax.rem(walk + d, 16), d):
            copy.wait()
        return carry

    lax.fori_loop(1, 16, place_start, 0)
    staged[walk] = whole[owner[walk]]
    mine = [
        pltpu.make_async_copy(
            staged.at[walk, ch], (out_c, out_h)[ch].at[pl.ds((row_c, row_h)[ch], 16), :], local_sem.at[ch]
        )
        for ch in range(2)
    ]
    for copy in mine:
        copy.start()
    for copy in gather:
        copy.wait_send()

    def sends(r, carry):
        for ch in range(2):
            for copy in ring1_of(r, ch) + ring2_of(r, ch):
                copy.wait_send()
        return carry

    lax.fori_loop(0, ROUNDS, sends, 0)
    for copy in mine:
        copy.wait()
    lax.fori_loop(1, 16, place_wait, 0)


def per_device(dlog, dener, energy, mask, owner):
    walkers, width = dlog.shape
    anywhere = pl.BlockSpec(memory_space=pl.ANY)
    scalars = pl.BlockSpec(memory_space=pltpu.SMEM)
    dma = pltpu.SemaphoreType.DMA
    out = jax.ShapeDtypeStruct((BLOCK, width), F32)
    return pl.pallas_call(
        kernel,
        out_shape=(out, out),
        in_specs=[scalars, scalars, anywhere, anywhere, pl.BlockSpec(memory_space=pltpu.VMEM)],
        out_specs=(anywhere, anywhere),
        scratch_shapes=[
            pltpu.VMEM((8, walkers, BLOCK), BF16),
            pltpu.VMEM((walkers, width), BF16),
            pltpu.VMEM((walkers, width), BF16),
            pltpu.VMEM((walkers, width), BF16),
            pltpu.VMEM((2, 4, walkers, BLOCK), BF16),
            pltpu.VMEM((2 * BLOCK, walkers), BF16),
            pltpu.VMEM((walkers, 128), F32),
            pltpu.VMEM((ROUNDS, 2, 2, 4, 2, 64, width), BF16),
            pltpu.VMEM((ROUNDS, 2, 6, 2, 64, width), BF16),
            pltpu.VMEM((ROUNDS, 2, 2, 4, 2, 16, width), BF16),
            pltpu.VMEM((ROUNDS, 2, 6, 2, 16, width), BF16),
            pltpu.VMEM((16, 2, 16, width), F32),
            pltpu.VMEM((ROUNDS, 2, 2, 16, width), F32),
            pltpu.VMEM((16, 2, 16, width), F32),
            pltpu.VMEM((16, 2, 8, BLOCK), F32),
            pltpu.VMEM((4, 2, 8, BLOCK), F32),
            pltpu.VMEM((2, 8, BLOCK), F32),
            dma((3,)), dma((6,)), dma((6,)), dma((2,)), dma((2,)), dma((16,)), dma((16,)), dma((4,)), dma((4,)),
            dma((ROUNDS, 2, 6)), dma((ROUNDS, 2, 6)), dma((ROUNDS, 2, 6)), dma((ROUNDS, 2, 6)),
            dma((ROUNDS, 2)), dma((ROUNDS, 2)), dma((16, 2)), dma((16, 2)),
        ],
        compiler_params=pltpu.CompilerParams(
            collective_id=0, has_side_effects=True, vmem_limit_bytes=64 * 1000 * 1000
        ),
    )(mask, owner, dlog, dener, energy.reshape(walkers // 128, 128))


def solution(mesh):
    return jax.shard_map(
        per_device,
        mesh=mesh,
        in_specs=(P("walk", "pan"), P("walk", "pan"), P("walk"), P(), P()),
        out_specs=(P("walk", "pan"), P("walk", "pan")),
        check_vma=False,
    )
```

```python
import jax
import jax.numpy as jnp
from jax import lax
from jax.experimental import pallas as pl
from jax.experimental.pallas import tpu as pltpu
from jax.sharding import PartitionSpec as P

BLOCK = 256
ROUNDS = 4
MESH = pl.DeviceIdType.MESH
F32 = jnp.float32
BF16 = jnp.bfloat16


def wrap4(v):
    return lax.rem(v, 4)


def kernel(
    mask, owner, dlog, dener, energy, out,
    blocks, gown, opar, gpar, right, left_t, spread,
    part, ring1, half, ring2, whole, give, staged, stats, means, pmeans,
    local_sem, ag_send, ag_recv, pt_send, pt_recv, st_send, st_recv, mm_send, mm_recv,
    r1_send, r1_recv, r2_send, r2_recv, z_send, z_recv, f_send, f_recv,
):
    walkers = dlog.shape[0]
    total = walkers * 16
    scale = 1.0 / total
    chunk = 256
    steps = walkers // chunk

    walk = lax.axis_index("walk")
    pan = lax.axis_index("pan")
    px, pz = lax.div(walk, 4), lax.rem(walk, 4)
    py, core = lax.div(pan, 2), lax.rem(pan, 2)
    partner = (walk, py * 2 + (1 - core))

    def at_y(shift):
        return (walk, wrap4(py + shift) * 2 + core)

    def remote(src, dst, send, recv, device):
        return pltpu.make_async_remote_copy(
            src_ref=src, dst_ref=dst, send_sem=send, recv_sem=recv, device_id=device, device_id_type=MESH
        )

    own = [
        pltpu.make_async_copy(dlog.at[:, pl.ds(b * BLOCK, BLOCK)], blocks.at[b], local_sem.at[b]) for b in range(2)
    ] + [pltpu.make_async_copy(dener, gown, local_sem.at[2])]
    for copy in own:
        copy.start()

    barrier = pltpu.get_barrier_semaphore()

    def greet(d, carry):
        pl.semaphore_signal(barrier, inc=1, device_id=(lax.rem(walk + d, 16), pan), device_id_type=MESH)
        return carry

    lax.fori_loop(1, 16, greet, 0)
    for d in range(1, 4):
        pl.semaphore_signal(barrier, inc=1, device_id=at_y(d), device_id_type=MESH)
    pl.semaphore_signal(barrier, inc=1, device_id=partner, device_id_type=MESH)
    pl.semaphore_wait(barrier, 19)

    def column(b):
        return dlog.at[:, pl.ds(b * BLOCK, BLOCK)]

    gather = [
        remote(column(0), blocks.at[2], ag_send.at[0], ag_recv.at[0], at_y(1)),
        remote(column(1), blocks.at[3], ag_send.at[1], ag_recv.at[1], at_y(3)),
        remote(column(1), blocks.at[4], ag_send.at[2], ag_recv.at[2], at_y(1)),
        remote(column(0), blocks.at[5], ag_send.at[3], ag_recv.at[3], at_y(3)),
        remote(blocks.at[2], blocks.at[6], ag_send.at[4], ag_recv.at[4], at_y(1)),
        remote(blocks.at[3], blocks.at[7], ag_send.at[5], ag_recv.at[5], at_y(3)),
    ]
    for copy in gather[:4]:
        copy.start()
    pair = [
        remote(dlog, opar, pt_send.at[0], pt_recv.at[0], partner),
        remote(dener, gpar, pt_send.at[1], pt_recv.at[1], partner),
    ]
    for copy in pair:
        copy.start()

    for copy in own:
        copy.wait()
    esum = jnp.sum(energy[...])
    for b in range(2):

        def add(i, carry):
            rows = pl.ds(pl.multiple_of(i * chunk, chunk), chunk)
            o = jnp.sum(blocks[b, rows, :].astype(F32), axis=0, keepdims=True)
            g = jnp.sum(gown[rows, b * BLOCK:(b + 1) * BLOCK].astype(F32), axis=0, keepdims=True)
            return carry[0] + o, carry[1] + g

        zero = jnp.zeros((1, BLOCK), F32)
        o, g = lax.fori_loop(0, steps, add, (zero, zero))
        stats[walk, b] = jnp.concatenate([o, g, jnp.full((1, BLOCK), esum, F32), jnp.zeros((5, BLOCK), F32)], axis=0)

    def stat_copy(d):
        return remote(
            stats.at[walk], stats.at[walk], st_send.at[d], st_recv.at[d], (lax.rem(walk + d, 16), pan)
        )

    def stat_start(d, carry):
        stat_copy(d).start()
        return carry

    def stat_wait(d, carry):
        stat_copy(d).wait()
        return carry

    lax.fori_loop(1, 16, stat_start, 0)
    lax.fori_loop(1, 16, stat_wait, 0)
    sums = stats[0]
    for i in range(1, 16):
        sums = sums + stats[i]
    means[py] = sums * scale
    shared = [remote(means.at[py], means.at[py], mm_send.at[d], mm_recv.at[d], at_y(d)) for d in range(1, 4)] + [
        remote(means.at[py], pmeans, mm_send.at[0], mm_recv.at[0], partner)
    ]
    for copy in shared:
        copy.start()

    ebar = means[py, 0, 2:3, 0:128]
    for i in range(walkers // 128):
        row = energy[i:i + 1, :] - ebar
        spread[i * 128:(i + 1) * 128, :] = jnp.broadcast_to(row, (128, 128)).T

    def build(o_of, g_of, obar, gbar, m, side, b):
        def step(i, carry):
            rows = pl.ds(pl.multiple_of(i * chunk, chunk), chunk)
            oc = o_of(rows).astype(F32) * m - obar
            e = spread[rows, :]
            hc = jnp.concatenate([e, e], axis=1) * oc + g_of(rows).astype(F32) * m - gbar
            right[0, side, b, rows, :] = oc.astype(BF16)
            right[1, side, b, rows, :] = hc.astype(BF16)
            return carry

        lax.fori_loop(0, steps, step, 0)

    def build_own():
        for b in range(2):
            m = mask[py * 4 + core * 2 + b].astype(F32)
            build(
                lambda rows, b=b: blocks[b, rows, :],
                lambda rows, b=b: gown[rows, b * BLOCK:(b + 1) * BLOCK],
                means[py, b, 0:1, :] * m,
                means[py, b, 1:2, :] * m,
                m,
                0,
                b,
            )

    def build_partner():
        for copy in pair:
            copy.wait()
        for copy in shared:
            copy.wait()
        for b in range(2):
            m = mask[py * 4 + (1 - core) * 2 + b].astype(F32)
            build(
                lambda rows, b=b: opar[rows, b * BLOCK:(b + 1) * BLOCK],
                lambda rows, b=b: gpar[rows, b * BLOCK:(b + 1) * BLOCK],
                pmeans[b, 0:1, :] * m,
                pmeans[b, 1:2, :] * m,
                m,
                1,
                b,
            )

    xs = (px, (wrap4(px + 1) * 4 + pz, pan), (wrap4(px + 3) * 4 + pz, pan))
    zs = (pz, (px * 4 + wrap4(pz + 1), pan), (px * 4 + wrap4(pz + 3), pan))

    def ring(buf, got, send, recv, axis):
        me, up, down = axis
        far, nxt, prv = wrap4(me + 2), wrap4(me + 1), wrap4(me + 3)
        return [
            remote(buf.at[0, far], got.at[0], send.at[0], recv.at[0], up),
            remote(buf.at[1, far], got.at[1], send.at[1], recv.at[1], down),
            remote(buf.at[1, nxt], got.at[2], send.at[2], recv.at[2], up),
            remote(buf.at[0, prv], got.at[3], send.at[3], recv.at[3], down),
            remote(buf.at[0, nxt], got.at[4], send.at[4], recv.at[4], up),
            remote(buf.at[1, prv], got.at[5], send.at[5], recv.at[5], down),
        ]

    chains = [(ch, side) for side in range(2) for ch in range(2)]
    arrivals = ((3, 4), (2, 5))

    def ring1_of(r, ch, side):
        at = (r, ch, side)
        return ring(part.at[at], ring1.at[at], r1_send.at[at], r1_recv.at[at], (xs, zs)[ch])

    def ring2_of(r, ch, side):
        at = (r, ch, side)
        return ring(half.at[at], ring2.at[at], r2_send.at[at], r2_recv.at[at], (zs, xs)[ch])

    def ring_start(copies):
        for copy in copies[:4]:
            copy.start()

    def ring_mid(copies, buf, got, axis):
        for b, shift in ((0, 1), (1, 3)):
            copies[b].wait_recv()
            k = wrap4(axis[0] + shift)
            buf[b, k] = (buf[b, k].astype(F32) + got[b].astype(F32)).astype(BF16)
            copies[4 + b].start()

    def mid1(r, ch, side):
        at = (r, ch, side)
        ring_mid(ring1_of(*at), part.at[at], ring1.at[at], (xs, zs)[ch])

    def mid2(r, ch, side):
        at = (r, ch, side)
        ring_mid(ring2_of(*at), half.at[at], ring2.at[at], (zs, xs)[ch])

    def reduced(r, ch, side, b, rows):
        i, j = arrivals[b]
        own = part[r, ch, side, b, (px, pz)[ch], rows, :].astype(F32)
        return own + ring1[r, ch, side, i, rows, :].astype(F32) + ring1[r, ch, side, j, rows, :].astype(F32)

    def fin1(r, ch, side):
        copies = ring1_of(r, ch, side)
        for b in range(2):
            for k in arrivals[b]:
                copies[k].wait_recv()
            for k in range(4):
                half[r, ch, side, b, k] = reduced(r, ch, side, b, slice(16 * k, 16 * k + 16)).astype(BF16)
        ring_start(ring2_of(r, ch, side))

    def fin2(r, ch, side):
        copies = ring2_of(r, ch, side)
        for b in range(2):
            i, j = arrivals[b]
            copies[i].wait_recv()
            copies[j].wait_recv()
            rows = pl.ds(pl.multiple_of((pz, px)[ch] * 16, 16), 16)
            got = ring2[r, ch, side, i].astype(F32) + ring2[r, ch, side, j].astype(F32)
            value = (reduced(r, ch, side, b, rows) + got) * scale
            if side == 0:
                whole[block_of(r, b), ch] = value
            else:
                give[r, b, ch] = value

    def source(r, b):
        step = ((0, 0), (3, 1), (3, 1), (2, 2))[r][b]
        return wrap4(py + step), (1 - b if r == 2 else b)

    def block_of(r, b):
        ysrc, bsel = source(r, b)
        return ysrc * 4 + core * 2 + bsel

    def give_copy(r, b):
        return remote(give.at[r, b], whole.at[block_of(r, b)], z_send.at[r, b], z_recv.at[r, b], partner)

    def gathered(r):
        for b in range(2):
            gather[2 * (r - 1) + b].wait_recv()
            if r == 1:
                gather[4 + b].start()

    def load_left(r):
        for b in range(2):
            ysrc, bsel = source(r, b)
            m = mask[ysrc * 4 + core * 2 + bsel].astype(F32)
            obar = means[ysrc, bsel, 0:1, :] * m

            def turn(i, c):
                rows = pl.ds(pl.multiple_of(i * chunk, chunk), chunk)
                oc = blocks[2 * r + b, rows, :].astype(F32) * m - obar
                left_t[b * BLOCK:(b + 1) * BLOCK, rows] = oc.T.astype(BF16)
                return c

            lax.fori_loop(0, steps, turn, 0)

    def multiply(r, ch, side):
        for b in range(2):
            product = jnp.dot(left_t[...], right[ch, side, b], preferred_element_type=F32)
            part[r, ch, side, :, :, :, b * BLOCK:(b + 1) * BLOCK] = product.astype(BF16).reshape(2, 4, 64, BLOCK)
        ring_start(ring1_of(r, ch, side))

    def finish(r):
        for ch, side in chains:
            fin2(r, ch, side)
        for b in range(2):
            give_copy(r, b).start()

    build_own()
    load_left(0)
    multiply(0, 0, 0)
    multiply(0, 1, 0)
    build_partner()
    multiply(0, 0, 1)
    multiply(0, 1, 1)
    for r in range(1, ROUNDS):
        if r > 1:
            for ch, side in chains:
                mid1(r - 1, ch, side)
            for ch, side in chains:
                fin1(r - 1, ch, side)
        gathered(r)
        load_left(r)
        multiply(r, 0, 0)
        if r == 1:
            for ch, side in chains:
                mid1(r - 1, ch, side)
        else:
            for ch, side in chains:
                mid2(r - 1, ch, side)
        multiply(r, 1, 0)
        if r == 1:
            for ch, side in chains:
                fin1(r - 1, ch, side)
        multiply(r, 0, 1)
        if r == 1:
            for ch, side in chains:
                mid2(r - 1, ch, side)
        multiply(r, 1, 1)
        finish(r - 1)
    last = ROUNDS - 1
    for step in (mid1, fin1, mid2):
        for ch, side in chains:
            step(last, ch, side)
    finish(last)

    for r in range(ROUNDS):
        for b in range(2):
            give_copy(r, b).wait()

    row_c = pl.multiple_of(px * 64 + pz * 16, 16)
    row_h = pl.multiple_of(pz * 64 + px * 16, 16)

    def place(r, d):
        return [
            remote(
                staged.at[r, ch],
                out.at[ch, pl.ds((row_c, row_h)[ch], 16), :],
                f_send.at[d, ch],
                f_recv.at[d, ch],
                (r, pan),
            )
            for ch in range(2)
        ]

    def place_start(d, carry):
        r = lax.rem(walk + d, 16)
        staged[r] = whole[owner[r]].astype(BF16)
        for copy in place(r, d):
            copy.start()
        return carry

    def place_wait(d, carry):
        for copy in place(lax.rem(walk + d, 16), d):
            copy.wait()
        return carry

    lax.fori_loop(1, 16, place_start, 0)
    staged[walk] = whole[owner[walk]].astype(BF16)
    mine = [
        pltpu.make_async_copy(
            staged.at[walk, ch], out.at[ch, pl.ds((row_c, row_h)[ch], 16), :], local_sem.at[ch]
        )
        for ch in range(2)
    ]
    for copy in mine:
        copy.start()
    for copy in gather:
        copy.wait_send()

    def sends(r, carry):
        for ch, side in chains:
            for copy in ring1_of(r, ch, side) + ring2_of(r, ch, side):
                copy.wait_send()
        return carry

    lax.fori_loop(0, ROUNDS, sends, 0)
    for copy in mine:
        copy.wait()
    lax.fori_loop(1, 16, place_wait, 0)


def per_device(dlog, dener, energy, mask, owner):
    walkers, width = dlog.shape
    anywhere = pl.BlockSpec(memory_space=pl.ANY)
    scalars = pl.BlockSpec(memory_space=pltpu.SMEM)
    dma = pltpu.SemaphoreType.DMA
    both = pl.pallas_call(
        kernel,
        out_shape=jax.ShapeDtypeStruct((2, BLOCK, width), BF16),
        in_specs=[scalars, scalars, anywhere, anywhere, pl.BlockSpec(memory_space=pltpu.VMEM)],
        out_specs=anywhere,
        scratch_shapes=[
            pltpu.VMEM((8, walkers, BLOCK), BF16),
            pltpu.VMEM((walkers, width), BF16),
            pltpu.VMEM((walkers, width), BF16),
            pltpu.VMEM((walkers, width), BF16),
            pltpu.VMEM((2, 2, 2, walkers, BLOCK), BF16),
            pltpu.VMEM((2 * BLOCK, walkers), BF16),
            pltpu.VMEM((walkers, 128), F32),
            pltpu.VMEM((ROUNDS, 2, 2, 2, 4, 64, width), BF16),
            pltpu.VMEM((ROUNDS, 2, 2, 6, 64, width), BF16),
            pltpu.VMEM((ROUNDS, 2, 2, 2, 4, 16, width), BF16),
            pltpu.VMEM((ROUNDS, 2, 2, 6, 16, width), BF16),
            pltpu.VMEM((16, 2, 16, width), F32),
            pltpu.VMEM((ROUNDS, 2, 2, 16, width), F32),
            pltpu.VMEM((16, 2, 16, width), BF16),
            pltpu.VMEM((16, 2, 8, BLOCK), F32),
            pltpu.VMEM((4, 2, 8, BLOCK), F32),
            pltpu.VMEM((2, 8, BLOCK), F32),
            dma((3,)), dma((6,)), dma((6,)), dma((2,)), dma((2,)), dma((16,)), dma((16,)), dma((4,)), dma((4,)),
            dma((ROUNDS, 2, 2, 6)), dma((ROUNDS, 2, 2, 6)), dma((ROUNDS, 2, 2, 6)), dma((ROUNDS, 2, 2, 6)),
            dma((ROUNDS, 2)), dma((ROUNDS, 2)), dma((16, 2)), dma((16, 2)),
        ],
        compiler_params=pltpu.CompilerParams(
            collective_id=0, has_side_effects=True, vmem_limit_bytes=64 * 1000 * 1000
        ),
    )(mask, owner, dlog, dener, energy.reshape(walkers // 128, 128))
    return both[0].astype(F32), both[1].astype(F32)


def solution(mesh):
    return jax.shard_map(
        per_device,
        mesh=mesh,
        in_specs=(P("walk", "pan"), P("walk", "pan"), P("walk"), P(), P()),
        out_specs=(P("walk", "pan"), P("walk", "pan")),
        check_vma=False,
    )
```

```python
import jax
import jax.numpy as jnp
from jax import lax
from jax.experimental import pallas as pl
from jax.experimental.pallas import tpu as pltpu
from jax.sharding import PartitionSpec as P

BLOCK = 256
ROUNDS = 4
MESH = pl.DeviceIdType.MESH
F32 = jnp.float32
BF16 = jnp.bfloat16


def wrap4(v):
    return lax.rem(v, 4)


def kernel(
    mask, owner, dlog, dener, energy, out,
    blocks, gown, opar, gpar, right, left_t, spread,
    part, ring1, half, ring2, whole, give, staged, stats, means, pmeans,
    local_sem, ag_send, ag_recv, pt_send, pt_recv, st_send, st_recv, mm_send, mm_recv,
    r1_send, r1_recv, r2_send, r2_recv, z_send, z_recv, f_send, f_recv,
):
    walkers = dlog.shape[0]
    total = walkers * 16
    scale = 1.0 / total
    chunk = 256
    steps = walkers // chunk

    walk = lax.axis_index("walk")
    pan = lax.axis_index("pan")
    px, pz = lax.div(walk, 4), lax.rem(walk, 4)
    py, core = lax.div(pan, 2), lax.rem(pan, 2)
    partner = (walk, py * 2 + (1 - core))

    def at_y(shift):
        return (walk, wrap4(py + shift) * 2 + core)

    def remote(src, dst, send, recv, device):
        return pltpu.make_async_remote_copy(
            src_ref=src, dst_ref=dst, send_sem=send, recv_sem=recv, device_id=device, device_id_type=MESH
        )

    own = [
        pltpu.make_async_copy(dlog.at[:, pl.ds(b * BLOCK, BLOCK)], blocks.at[b], local_sem.at[b]) for b in range(2)
    ] + [pltpu.make_async_copy(dener, gown, local_sem.at[2])]
    for copy in own:
        copy.start()

    barrier = pltpu.get_barrier_semaphore()

    near = [
        (wrap4(px + 1) * 4 + pz, pan),
        (wrap4(px + 3) * 4 + pz, pan),
        (px * 4 + wrap4(pz + 1), pan),
        (px * 4 + wrap4(pz + 3), pan),
        at_y(1),
        at_y(3),
        partner,
    ]
    for device in near:
        pl.semaphore_signal(barrier, inc=1, device_id=device, device_id_type=MESH)
    pl.semaphore_wait(barrier, len(near))

    def column(b):
        return dlog.at[:, pl.ds(b * BLOCK, BLOCK)]

    gather = [
        remote(column(0), blocks.at[2], ag_send.at[0], ag_recv.at[0], at_y(1)),
        remote(column(1), blocks.at[3], ag_send.at[1], ag_recv.at[1], at_y(3)),
        remote(column(1), blocks.at[4], ag_send.at[2], ag_recv.at[2], at_y(1)),
        remote(column(0), blocks.at[5], ag_send.at[3], ag_recv.at[3], at_y(3)),
        remote(blocks.at[2], blocks.at[6], ag_send.at[4], ag_recv.at[4], at_y(1)),
        remote(blocks.at[3], blocks.at[7], ag_send.at[5], ag_recv.at[5], at_y(3)),
    ]
    for copy in gather[:2]:
        copy.start()
    pair = [
        remote(dlog, opar, pt_send.at[0], pt_recv.at[0], partner),
        remote(dener, gpar, pt_send.at[1], pt_recv.at[1], partner),
    ]
    for copy in pair:
        copy.start()

    for copy in own:
        copy.wait()
    esum = jnp.sum(energy[...])
    for b in range(2):

        def add(i, carry):
            rows = pl.ds(pl.multiple_of(i * chunk, chunk), chunk)
            o = jnp.sum(blocks[b, rows, :].astype(F32), axis=0, keepdims=True)
            g = jnp.sum(gown[rows, b * BLOCK:(b + 1) * BLOCK].astype(F32), axis=0, keepdims=True)
            return carry[0] + o, carry[1] + g

        zero = jnp.zeros((1, BLOCK), F32)
        o, g = lax.fori_loop(0, steps, add, (zero, zero))
        stats[0, 0, b] = jnp.concatenate([o, g, jnp.full((1, BLOCK), esum, F32), jnp.zeros((5, BLOCK), F32)], axis=0)

    swaps = [
        ((px + 1 - 2 * lax.rem(px, 2)) * 4 + pz, pan),
        ((3 - px) * 4 + pz, pan),
        (px * 4 + pz + 1 - 2 * lax.rem(pz, 2), pan),
        (px * 4 + 3 - pz, pan),
    ]
    for n, device in enumerate(swaps):
        swap = remote(stats.at[0, n], stats.at[1, n], st_send.at[n], st_recv.at[n], device)
        swap.start()
        swap.wait()
        stats[0, n + 1] = stats[0, n] + stats[1, n]
    means[py] = stats[0, 4] * scale
    below = wrap4(py + 3)
    shared = [
        remote(means.at[py], means.at[py], mm_send.at[0], mm_recv.at[0], at_y(1)),
        remote(means.at[py], means.at[py], mm_send.at[1], mm_recv.at[1], at_y(3)),
        remote(means.at[below], means.at[below], mm_send.at[2], mm_recv.at[2], at_y(1)),
        remote(means.at[py], pmeans, mm_send.at[3], mm_recv.at[3], partner),
    ]
    for copy in [shared[0], shared[1], shared[3]] + gather[2:4]:
        copy.start()

    ebar = means[py, 0, 2:3, 0:128]
    for i in range(walkers // 128):
        row = energy[i:i + 1, :] - ebar
        spread[i * 128:(i + 1) * 128, :] = jnp.broadcast_to(row, (128, 128)).T

    def build(o_of, g_of, obar, gbar, m, side, b):
        def step(i, carry):
            rows = pl.ds(pl.multiple_of(i * chunk, chunk), chunk)
            oc = o_of(rows).astype(F32) * m - obar
            e = spread[rows, :]
            hc = jnp.concatenate([e, e], axis=1) * oc + g_of(rows).astype(F32) * m - gbar
            right[0, side, b, rows, :] = oc.astype(BF16)
            right[1, side, b, rows, :] = hc.astype(BF16)
            return carry

        lax.fori_loop(0, steps, step, 0)

    def build_own():
        for b in range(2):
            m = mask[py * 4 + core * 2 + b].astype(F32)
            build(
                lambda rows, b=b: blocks[b, rows, :],
                lambda rows, b=b: gown[rows, b * BLOCK:(b + 1) * BLOCK],
                means[py, b, 0:1, :] * m,
                means[py, b, 1:2, :] * m,
                m,
                0,
                b,
            )

    def build_partner():
        for copy in pair:
            copy.wait()
        shared[3].wait()
        for b in range(2):
            m = mask[py * 4 + (1 - core) * 2 + b].astype(F32)
            build(
                lambda rows, b=b: opar[rows, b * BLOCK:(b + 1) * BLOCK],
                lambda rows, b=b: gpar[rows, b * BLOCK:(b + 1) * BLOCK],
                pmeans[b, 0:1, :] * m,
                pmeans[b, 1:2, :] * m,
                m,
                1,
                b,
            )

    xs = (px, (wrap4(px + 1) * 4 + pz, pan), (wrap4(px + 3) * 4 + pz, pan))
    zs = (pz, (px * 4 + wrap4(pz + 1), pan), (px * 4 + wrap4(pz + 3), pan))

    def ring(buf, got, send, recv, axis):
        me, up, down = axis
        far, nxt, prv = wrap4(me + 2), wrap4(me + 1), wrap4(me + 3)
        return [
            remote(buf.at[0, far], got.at[0], send.at[0], recv.at[0], up),
            remote(buf.at[1, far], got.at[1], send.at[1], recv.at[1], down),
            remote(buf.at[1, nxt], got.at[2], send.at[2], recv.at[2], up),
            remote(buf.at[0, prv], got.at[3], send.at[3], recv.at[3], down),
            remote(buf.at[0, nxt], got.at[4], send.at[4], recv.at[4], up),
            remote(buf.at[1, prv], got.at[5], send.at[5], recv.at[5], down),
        ]

    chains = [(ch, side) for side in range(2) for ch in range(2)]
    arrivals = ((3, 4), (2, 5))

    def ring1_of(r, ch, side):
        at = (r, ch, side)
        return ring(part.at[at], ring1.at[at], r1_send.at[at], r1_recv.at[at], (xs, zs)[ch])

    def ring2_of(r, ch, side):
        at = (r, ch, side)
        return ring(half.at[at], ring2.at[at], r2_send.at[at], r2_recv.at[at], (zs, xs)[ch])

    def ring_start(copies):
        for copy in copies[:4]:
            copy.start()

    def ring_mid(copies, buf, got, axis):
        for b, shift in ((0, 1), (1, 3)):
            copies[b].wait_recv()
            k = wrap4(axis[0] + shift)
            buf[b, k] = (buf[b, k].astype(F32) + got[b].astype(F32)).astype(BF16)
            copies[4 + b].start()

    def mid1(r, ch, side):
        at = (r, ch, side)
        ring_mid(ring1_of(*at), part.at[at], ring1.at[at], (xs, zs)[ch])

    def mid2(r, ch, side):
        at = (r, ch, side)
        ring_mid(ring2_of(*at), half.at[at], ring2.at[at], (zs, xs)[ch])

    def reduced(r, ch, side, b, rows):
        i, j = arrivals[b]
        own = part[r, ch, side, b, (px, pz)[ch], rows, :].astype(F32)
        return own + ring1[r, ch, side, i, rows, :].astype(F32) + ring1[r, ch, side, j, rows, :].astype(F32)

    def fin1(r, ch, side):
        copies = ring1_of(r, ch, side)
        for b in range(2):
            for k in arrivals[b]:
                copies[k].wait_recv()
            for k in range(4):
                half[r, ch, side, b, k] = reduced(r, ch, side, b, slice(16 * k, 16 * k + 16)).astype(BF16)
        ring_start(ring2_of(r, ch, side))

    def fin2(r, ch, side):
        copies = ring2_of(r, ch, side)
        for b in range(2):
            i, j = arrivals[b]
            copies[i].wait_recv()
            copies[j].wait_recv()
            rows = pl.ds(pl.multiple_of((pz, px)[ch] * 16, 16), 16)
            got = ring2[r, ch, side, i].astype(F32) + ring2[r, ch, side, j].astype(F32)
            value = (reduced(r, ch, side, b, rows) + got) * scale
            if side == 0:
                whole[block_of(r, b), ch] = value
            else:
                give[r, b, ch] = value

    def source(r, b):
        step = ((0, 0), (3, 1), (3, 1), (2, 2))[r][b]
        return wrap4(py + step), (1 - b if r == 2 else b)

    def block_of(r, b):
        ysrc, bsel = source(r, b)
        return ysrc * 4 + core * 2 + bsel

    def give_copy(r, b):
        return remote(give.at[r, b], whole.at[block_of(r, b)], z_send.at[r, b], z_recv.at[r, b], partner)

    def gathered(r):
        for k in ((0, 1), (), (2,))[r - 1]:
            shared[k].wait_recv()
        if r == 1:
            shared[2].start()
        for b in range(2):
            gather[2 * (r - 1) + b].wait_recv()
            if r == 1:
                gather[4 + b].start()

    def load_left(r):
        for b in range(2):
            ysrc, bsel = source(r, b)
            m = mask[ysrc * 4 + core * 2 + bsel].astype(F32)
            obar = means[ysrc, bsel, 0:1, :] * m

            def turn(i, c):
                rows = pl.ds(pl.multiple_of(i * chunk, chunk), chunk)
                oc = blocks[2 * r + b, rows, :].astype(F32) * m - obar
                left_t[b * BLOCK:(b + 1) * BLOCK, rows] = oc.T.astype(BF16)
                return c

            lax.fori_loop(0, steps, turn, 0)

    def multiply(r, ch, side):
        for b in range(2):
            product = jnp.dot(left_t[...], right[ch, side, b], preferred_element_type=F32)
            part[r, ch, side, :, :, :, b * BLOCK:(b + 1) * BLOCK] = product.astype(BF16).reshape(2, 4, 64, BLOCK)
        ring_start(ring1_of(r, ch, side))

    def finish(r):
        for ch, side in chains:
            fin2(r, ch, side)
        for b in range(2):
            give_copy(r, b).start()

    build_own()
    load_left(0)
    multiply(0, 0, 0)
    multiply(0, 1, 0)
    build_partner()
    multiply(0, 0, 1)
    multiply(0, 1, 1)
    for r in range(1, ROUNDS):
        if r > 1:
            for ch, side in chains:
                mid1(r - 1, ch, side)
            for ch, side in chains:
                fin1(r - 1, ch, side)
        gathered(r)
        load_left(r)
        multiply(r, 0, 0)
        if r == 1:
            for ch, side in chains:
                mid1(r - 1, ch, side)
        else:
            for ch, side in chains:
                mid2(r - 1, ch, side)
        multiply(r, 1, 0)
        if r == 1:
            for ch, side in chains:
                fin1(r - 1, ch, side)
        multiply(r, 0, 1)
        if r == 1:
            for ch, side in chains:
                mid2(r - 1, ch, side)
        multiply(r, 1, 1)
        finish(r - 1)
    last = ROUNDS - 1
    for step in (mid1, fin1, mid2):
        for ch, side in chains:
            step(last, ch, side)
    finish(last)

    for r in range(ROUNDS):
        for b in range(2):
            give_copy(r, b).wait()

    row_c = pl.multiple_of(px * 64 + pz * 16, 16)
    row_h = pl.multiple_of(pz * 64 + px * 16, 16)

    def place(r, d):
        return [
            remote(
                staged.at[r, ch],
                out.at[ch, pl.ds((row_c, row_h)[ch], 16), :],
                f_send.at[d, ch],
                f_recv.at[d, ch],
                (r, pan),
            )
            for ch in range(2)
        ]

    def place_start(d, carry):
        r = lax.rem(walk + d, 16)
        staged[r] = whole[owner[r]].astype(BF16)
        for copy in place(r, d):
            copy.start()
        return carry

    def place_wait(d, carry):
        for copy in place(lax.rem(walk + d, 16), d):
            copy.wait()
        return carry

    lax.fori_loop(1, 16, place_start, 0)
    staged[walk] = whole[owner[walk]].astype(BF16)
    mine = [
        pltpu.make_async_copy(
            staged.at[walk, ch], out.at[ch, pl.ds((row_c, row_h)[ch], 16), :], local_sem.at[ch]
        )
        for ch in range(2)
    ]
    for copy in mine:
        copy.start()
    for copy in gather + shared[:3]:
        copy.wait_send()

    def sends(r, carry):
        for ch, side in chains:
            for copy in ring1_of(r, ch, side) + ring2_of(r, ch, side):
                copy.wait_send()
        return carry

    lax.fori_loop(0, ROUNDS, sends, 0)
    for copy in mine:
        copy.wait()
    lax.fori_loop(1, 16, place_wait, 0)


def per_device(dlog, dener, energy, mask, owner):
    walkers, width = dlog.shape
    anywhere = pl.BlockSpec(memory_space=pl.ANY)
    scalars = pl.BlockSpec(memory_space=pltpu.SMEM)
    dma = pltpu.SemaphoreType.DMA
    both = pl.pallas_call(
        kernel,
        out_shape=jax.ShapeDtypeStruct((2, BLOCK, width), BF16),
        in_specs=[scalars, scalars, anywhere, anywhere, pl.BlockSpec(memory_space=pltpu.VMEM)],
        out_specs=anywhere,
        scratch_shapes=[
            pltpu.VMEM((8, walkers, BLOCK), BF16),
            pltpu.VMEM((walkers, width), BF16),
            pltpu.VMEM((walkers, width), BF16),
            pltpu.VMEM((walkers, width), BF16),
            pltpu.VMEM((2, 2, 2, walkers, BLOCK), BF16),
            pltpu.VMEM((2 * BLOCK, walkers), BF16),
            pltpu.VMEM((walkers, 128), F32),
            pltpu.VMEM((ROUNDS, 2, 2, 2, 4, 64, width), BF16),
            pltpu.VMEM((ROUNDS, 2, 2, 6, 64, width), BF16),
            pltpu.VMEM((ROUNDS, 2, 2, 2, 4, 16, width), BF16),
            pltpu.VMEM((ROUNDS, 2, 2, 6, 16, width), BF16),
            pltpu.VMEM((16, 2, 16, width), F32),
            pltpu.VMEM((ROUNDS, 2, 2, 16, width), F32),
            pltpu.VMEM((16, 2, 16, width), BF16),
            pltpu.VMEM((2, 5, 2, 8, BLOCK), F32),
            pltpu.VMEM((4, 2, 8, BLOCK), F32),
            pltpu.VMEM((2, 8, BLOCK), F32),
            dma((3,)), dma((6,)), dma((6,)), dma((2,)), dma((2,)), dma((4,)), dma((4,)), dma((4,)), dma((4,)),
            dma((ROUNDS, 2, 2, 6)), dma((ROUNDS, 2, 2, 6)), dma((ROUNDS, 2, 2, 6)), dma((ROUNDS, 2, 2, 6)),
            dma((ROUNDS, 2)), dma((ROUNDS, 2)), dma((16, 2)), dma((16, 2)),
        ],
        compiler_params=pltpu.CompilerParams(
            collective_id=0, has_side_effects=True, vmem_limit_bytes=64 * 1000 * 1000
        ),
    )(mask, owner, dlog, dener, energy.reshape(walkers // 128, 128))
    return both[0].astype(F32), both[1].astype(F32)


def solution(mesh):
    return jax.shard_map(
        per_device,
        mesh=mesh,
        in_specs=(P("walk", "pan"), P("walk", "pan"), P("walk"), P(), P()),
        out_specs=(P("walk", "pan"), P("walk", "pan")),
        check_vma=False,
    )
```

```python
import jax
import jax.numpy as jnp
from jax import lax
from jax.experimental import pallas as pl
from jax.experimental.pallas import tpu as pltpu
from jax.sharding import PartitionSpec as P

BLOCK = 256
ROUNDS = 5
PAIRS = 3
MESH = pl.DeviceIdType.MESH
F32 = jnp.float32
BF16 = jnp.bfloat16


def wrap4(v):
    return lax.rem(v, 4)


def kernel(
    mask_in, owner_in, dlog, dener, energy_in, out,
    mask, owner, energy,
    blocks, gown, opar, gpar, right, left_t, spread,
    part, ring1, half, ring2, part_s, ring1_s, half_s, ring2_s,
    near2, cross2, whole_c, whole_h, give, staged, stats, means, pmeans,
    local_sem, ag_send, ag_recv, pt_send, pt_recv, st_send, st_recv, mm_send, mm_recv,
    r1_send, r1_recv, r2_send, r2_recv, z_send, z_recv, f_send, f_recv,
    n2_send, n2_recv, c2_send, c2_recv,
):
    walkers = dlog.shape[0]
    total = walkers * 16
    scale = 1.0 / total
    chunk = 256
    steps = walkers // chunk

    walk = lax.axis_index("walk")
    pan = lax.axis_index("pan")
    px, pz = lax.div(walk, 4), lax.rem(walk, 4)
    py, core = lax.div(pan, 2), lax.rem(pan, 2)
    partner = (walk, py * 2 + (1 - core))

    def at_y(shift):
        return (walk, wrap4(py + shift) * 2 + core)

    def remote(src, dst, send, recv, device):
        return pltpu.make_async_remote_copy(
            src_ref=src, dst_ref=dst, send_sem=send, recv_sem=recv, device_id=device, device_id_type=MESH
        )

    barrier = pltpu.get_barrier_semaphore()

    near = [
        (wrap4(px + 1) * 4 + pz, pan),
        (wrap4(px + 3) * 4 + pz, pan),
        (px * 4 + wrap4(pz + 1), pan),
        (px * 4 + wrap4(pz + 3), pan),
        at_y(1),
        at_y(3),
        partner,
    ]
    for device in near:
        pl.semaphore_signal(barrier, inc=1, device_id=device, device_id_type=MESH)
    small = [
        pltpu.make_async_copy(source, target, local_sem.at[3 + n])
        for n, (source, target) in enumerate(((mask_in, mask), (owner_in, owner), (energy_in, energy)))
    ]
    own = [
        pltpu.make_async_copy(dlog.at[:, pl.ds(b * BLOCK, BLOCK)], blocks.at[b], local_sem.at[b]) for b in range(2)
    ] + [pltpu.make_async_copy(dener, gown, local_sem.at[2])]
    pl.semaphore_wait(barrier, len(near))

    def column(b):
        return dlog.at[:, pl.ds(b * BLOCK, BLOCK)]

    def onward(n, slot, to):
        rows = pl.ds((slot % 2) * (walkers // 2), walkers // 2)
        return remote(
            blocks.at[slot, rows, :], blocks.at[to, rows, :], ag_send.at[n], ag_recv.at[n], at_y(3 if slot % 2 else 1)
        )

    gather = [
        remote(column(0), blocks.at[2], ag_send.at[0], ag_recv.at[0], at_y(1)),
        remote(column(0), blocks.at[3], ag_send.at[1], ag_recv.at[1], at_y(3)),
        remote(column(1), blocks.at[4], ag_send.at[2], ag_recv.at[2], at_y(1)),
        remote(column(1), blocks.at[5], ag_send.at[3], ag_recv.at[3], at_y(3)),
        onward(4, 2, 6),
        onward(5, 3, 6),
        onward(6, 4, 7),
        onward(7, 5, 7),
    ]
    for copy in gather[:2] + own + small:
        copy.start()
    pair = [
        remote(dlog, opar, pt_send.at[0], pt_recv.at[0], partner),
        remote(dener, gpar, pt_send.at[1], pt_recv.at[1], partner),
    ]
    for copy in pair:
        copy.start()

    for copy in own + small:
        copy.wait()
    esum = jnp.sum(energy[...])
    for b in range(2):

        def add(i, carry):
            rows = pl.ds(pl.multiple_of(i * chunk, chunk), chunk)
            o = jnp.sum(blocks[b, rows, :].astype(F32), axis=0, keepdims=True)
            g = jnp.sum(gown[rows, b * BLOCK:(b + 1) * BLOCK].astype(F32), axis=0, keepdims=True)
            return carry[0] + o, carry[1] + g

        zero = jnp.zeros((1, BLOCK), F32)
        o, g = lax.fori_loop(0, steps, add, (zero, zero))
        stats[0, 0, b] = jnp.concatenate([o, g, jnp.full((1, BLOCK), esum, F32), jnp.zeros((5, BLOCK), F32)], axis=0)

    swaps = [
        ((px + 1 - 2 * lax.rem(px, 2)) * 4 + pz, pan),
        ((3 - px) * 4 + pz, pan),
        (px * 4 + pz + 1 - 2 * lax.rem(pz, 2), pan),
        (px * 4 + 3 - pz, pan),
    ]
    for n, device in enumerate(swaps):
        swap = remote(stats.at[0, n], stats.at[1, n], st_send.at[n], st_recv.at[n], device)
        swap.start()
        swap.wait()
        stats[0, n + 1] = stats[0, n] + stats[1, n]
    means[py] = stats[0, 4] * scale
    below = wrap4(py + 3)
    shared = [
        remote(means.at[py], means.at[py], mm_send.at[0], mm_recv.at[0], at_y(1)),
        remote(means.at[py], means.at[py], mm_send.at[1], mm_recv.at[1], at_y(3)),
        remote(means.at[below], means.at[below], mm_send.at[2], mm_recv.at[2], at_y(1)),
        remote(means.at[py], pmeans, mm_send.at[3], mm_recv.at[3], partner),
    ]
    for copy in [shared[0], shared[1], shared[3]] + gather[2:4]:
        copy.start()

    ebar = means[py, 0, 2:3, 0:128]
    for i in range(walkers // 128):
        row = energy[i:i + 1, :] - ebar
        spread[i * 128:(i + 1) * 128, :] = jnp.broadcast_to(row, (128, 128)).T

    def build(o_of, g_of, obar, gbar, m, side, b):
        def step(i, carry):
            rows = pl.ds(pl.multiple_of(i * chunk, chunk), chunk)
            oc = o_of(rows).astype(F32) * m - obar
            e = spread[rows, :]
            hc = jnp.concatenate([e, e], axis=1) * oc + g_of(rows).astype(F32) * m - gbar
            right[0, side, b, rows, :] = oc.astype(BF16)
            right[1, side, b, rows, :] = hc.astype(BF16)
            return carry

        lax.fori_loop(0, steps, step, 0)

    def build_own():
        for b in range(2):
            m = mask[py * 4 + core * 2 + b].astype(F32)
            build(
                lambda rows, b=b: blocks[b, rows, :],
                lambda rows, b=b: gown[rows, b * BLOCK:(b + 1) * BLOCK],
                means[py, b, 0:1, :] * m,
                means[py, b, 1:2, :] * m,
                m,
                0,
                b,
            )

    def build_partner():
        for copy in pair:
            copy.wait()
        shared[3].wait()
        for b in range(2):
            m = mask[py * 4 + (1 - core) * 2 + b].astype(F32)
            build(
                lambda rows, b=b: opar[rows, b * BLOCK:(b + 1) * BLOCK],
                lambda rows, b=b: gpar[rows, b * BLOCK:(b + 1) * BLOCK],
                pmeans[b, 0:1, :] * m,
                pmeans[b, 1:2, :] * m,
                m,
                1,
                b,
            )

    xs = (px, (wrap4(px + 1) * 4 + pz, pan), (wrap4(px + 3) * 4 + pz, pan))
    zs = (pz, (px * 4 + wrap4(pz + 1), pan), (px * 4 + wrap4(pz + 3), pan))

    def ring(buf, got, send, recv, axis):
        me, up, down = axis
        far, nxt, prv = wrap4(me + 2), wrap4(me + 1), wrap4(me + 3)
        return [
            remote(buf.at[0, far], got.at[0], send.at[0], recv.at[0], up),
            remote(buf.at[1, far], got.at[1], send.at[1], recv.at[1], down),
            remote(buf.at[1, nxt], got.at[2], send.at[2], recv.at[2], up),
            remote(buf.at[0, prv], got.at[3], send.at[3], recv.at[3], down),
            remote(buf.at[0, nxt], got.at[4], send.at[4], recv.at[4], up),
            remote(buf.at[1, prv], got.at[5], send.at[5], recv.at[5], down),
        ]

    last = ROUNDS - 1
    chains = [(ch, side) for side in range(2) for ch in range(2)]
    arrivals = ((3, 4), (2, 5))

    def buffers(r):
        return (part, ring1, half, ring2, r) if r < PAIRS else (part_s, ring1_s, half_s, ring2_s, r - PAIRS)

    def ring1_of(r, ch, side):
        buf, got, _, _, n = buffers(r)
        sems = (r, ch, side)
        return ring(buf.at[n, ch, side], got.at[n, ch, side], r1_send.at[sems], r1_recv.at[sems], (xs, zs)[ch])

    def ring2_of(r, ch, side):
        _, _, buf, got, n = buffers(r)
        sems = (r, ch, side)
        return ring(buf.at[n, ch, side], got.at[n, ch, side], r2_send.at[sems], r2_recv.at[sems], (zs, xs)[ch])

    def ring_start(copies):
        for copy in copies[:4]:
            copy.start()

    def ring_mid(copies, buf, got, axis):
        for b, shift in ((0, 1), (1, 3)):
            copies[b].wait_recv()
            k = wrap4(axis[0] + shift)
            buf[b, k] = (buf[b, k].astype(F32) + got[b].astype(F32)).astype(BF16)
            copies[4 + b].start()

    def mid1(r, ch, side):
        buf, got, _, _, n = buffers(r)
        ring_mid(ring1_of(r, ch, side), buf.at[n, ch, side], got.at[n, ch, side], (xs, zs)[ch])

    def mid2(r, ch, side):
        _, _, buf, got, n = buffers(r)
        ring_mid(ring2_of(r, ch, side), buf.at[n, ch, side], got.at[n, ch, side], (zs, xs)[ch])

    def reduced(r, ch, side, b, rows):
        buf, got, _, _, n = buffers(r)
        i, j = arrivals[b]
        own = buf[n, ch, side, b, (px, pz)[ch], rows, :].astype(F32)
        return own + got[n, ch, side, i, rows, :].astype(F32) + got[n, ch, side, j, rows, :].astype(F32)

    def fin1(r, ch, side):
        copies = ring1_of(r, ch, side)
        _, _, buf, _, n = buffers(r)
        for b in range(2):
            for k in arrivals[b]:
                copies[k].wait_recv()
            for k in range(4):
                buf[n, ch, side, b, k] = reduced(r, ch, side, b, slice(16 * k, 16 * k + 16)).astype(BF16)
        if r < last:
            ring_start(ring2_of(r, ch, side))
        else:
            for copy in direct2(ch, side):
                copy.start()

    def direct2(ch, side):
        me = (pz, px)[ch]
        copies = []
        for d in range(1 - side, 4):
            k = wrap4(me + d)
            device = ((px * 4 + k, k * 4 + pz)[ch], py * 2 + (1 - core if side else core))
            copies.append(
                remote(
                    half_s.at[last - PAIRS, ch, side, :, k],
                    (near2, cross2)[side].at[ch, d],
                    (n2_send, c2_send)[side].at[ch, d],
                    (n2_recv, c2_recv)[side].at[ch, d],
                    device,
                )
            )
        return copies

    def fin2_last(ch):
        order = last + PAIRS
        ysrc, bsel = source(order)
        rows = pl.ds(pl.multiple_of((pz, px)[ch] * 16, 16), 16)
        for side in range(2):
            for copy in direct2(ch, side):
                copy.wait_recv()
            for b in range(2):
                value = near2[ch, 1, b].astype(F32) if side == 0 else cross2[ch, 1, b].astype(F32)
                for d in (2, 3):
                    value = value + (near2, cross2)[side][ch, d, b].astype(F32)
                value = value + (reduced(last, ch, 0, b, rows) if side == 0 else cross2[ch, 0, b].astype(F32))
                block = ysrc * 4 + (1 - core if side else core) * 2 + bsel
                whole[ch][block, :, b * BLOCK:(b + 1) * BLOCK] = value * scale

    def fin2(r, ch, side):
        copies = ring2_of(r, ch, side)
        _, _, _, ring, n = buffers(r)
        for b in range(2):
            i, j = arrivals[b]
            copies[i].wait_recv()
            copies[j].wait_recv()
            rows = pl.ds(pl.multiple_of((pz, px)[ch] * 16, 16), 16)
            got = ring[n, ch, side, i].astype(F32) + ring[n, ch, side, j].astype(F32)
            value = (reduced(r, ch, side, b, rows) + got) * scale
            order = 2 * r + b if r < PAIRS else r + PAIRS
            lanes = slice(0, 2 * BLOCK) if r < PAIRS else slice(b * BLOCK, (b + 1) * BLOCK)
            if side == 0:
                whole[ch][block_of(order), :, lanes] = value
            else:
                give[order, ch, :, lanes] = value

    whole = (whole_c, whole_h)
    meets = ((0, 0), (0, 1), (3, 0), (1, 0), (3, 1), (1, 1), (2, 0), (2, 1))

    def source(order):
        return wrap4(py + meets[order][0]), meets[order][1]

    def block_of(order):
        ysrc, bsel = source(order)
        return ysrc * 4 + core * 2 + bsel

    def orders(r):
        return (2 * r, 2 * r + 1) if r < PAIRS else (r + PAIRS,)

    def give_copy(order, ch):
        return remote(
            give.at[order, ch], whole[ch].at[block_of(order)], z_send.at[order, ch], z_recv.at[order, ch], partner
        )

    def gathered(r):
        for k in ((0, 1), (), (2,), ())[r - 1]:
            shared[k].wait_recv()
        if r == 1:
            shared[2].start()
        for b in range(2):
            gather[2 * (r - 1) + b].wait_recv()
            if r <= 2:
                gather[2 * (r + 1) + b].start()

    def load_left(r):
        for b, order in enumerate(orders(r)):
            ysrc, bsel = source(order)
            m = mask[ysrc * 4 + core * 2 + bsel].astype(F32)
            obar = means[ysrc, bsel, 0:1, :] * m

            def turn(i, c):
                rows = pl.ds(pl.multiple_of(i * chunk, chunk), chunk)
                oc = blocks[order, rows, :].astype(F32) * m - obar
                left_t[b * BLOCK:(b + 1) * BLOCK, rows] = oc.T.astype(BF16)
                return c

            lax.fori_loop(0, steps, turn, 0)

    def multiply(r, ch, side):
        for b in range(2):
            if r < PAIRS:
                product = jnp.dot(left_t[...], right[ch, side, b], preferred_element_type=F32).astype(BF16)
                part[r, ch, side, :, :, :, b * BLOCK:(b + 1) * BLOCK] = product.reshape(2, 4, 64, BLOCK)
            else:
                product = jnp.dot(left_t[:BLOCK, :], right[ch, side, b], preferred_element_type=F32).astype(BF16)
                part_s[r - PAIRS, ch, side, b] = product.reshape(4, 64, BLOCK)
        ring_start(ring1_of(r, ch, side))

    def finish(r, ch):
        for side in range(2):
            fin2(r, ch, side)
        for order in orders(r):
            give_copy(order, ch).start()

    build_own()
    load_left(0)
    multiply(0, 0, 0)
    multiply(0, 1, 0)
    build_partner()
    multiply(0, 0, 1)
    multiply(0, 1, 1)
    def every(step, r):
        for ch, side in chains:
            step(r, ch, side)

    def finish_both(r):
        finish(r, 0)
        finish(r, 1)

    between = {
        1: (lambda: every(mid1, 0), None, lambda: every(fin1, 0), None),
        2: (lambda: every(mid2, 1), None, lambda: finish_both(1), None),
        3: (None, None, None, None),
        4: (lambda: every(mid2, 2), lambda: every(fin1, 3), lambda: finish_both(2), None),
    }
    after = {
        1: ((every, mid2, 0), (finish_both, 0), (every, mid1, 1), (every, fin1, 1)),
        2: (),
        3: ((every, mid1, 2), (every, fin1, 2), (every, mid1, 3)),
        4: ((every, mid1, 4), (every, mid2, 3)),
    }
    for r in range(1, ROUNDS):
        gathered(r)
        load_left(r)
        for (ch, side), also in zip(((0, 0), (0, 1), (1, 0), (1, 1)), between[r]):
            multiply(r, ch, side)
            if also is not None:
                also()
        for call, *arguments in after[r]:
            call(*arguments)

    row_c = pl.multiple_of(px * 64 + pz * 16, 16)
    row_h = pl.multiple_of(pz * 64 + px * 16, 16)

    def place(r, d, ch):
        return remote(
            staged.at[ch, r],
            out.at[ch, pl.ds((row_c, row_h)[ch], 16), :],
            f_send.at[d, ch],
            f_recv.at[d, ch],
            (r, pan),
        )

    mine = [
        pltpu.make_async_copy(
            staged.at[ch, walk], out.at[ch, pl.ds((row_c, row_h)[ch], 16), :], local_sem.at[ch]
        )
        for ch in range(2)
    ]

    def place_start(ch):
        for order in range(last + PAIRS):
            give_copy(order, ch).wait()

        def step(d, carry):
            r = lax.rem(walk + d, 16)
            staged[ch, r] = whole[ch][owner[r]].astype(BF16)
            place(r, d, ch).start()
            return carry

        lax.fori_loop(1, 16, step, 0)
        staged[ch, walk] = whole[ch][owner[walk]].astype(BF16)
        mine[ch].start()

    def place_wait(ch):
        def step(d, carry):
            place(lax.rem(walk + d, 16), d, ch).wait()
            return carry

        lax.fori_loop(1, 16, step, 0)

    by_output = [(0, 0), (0, 1), (1, 0), (1, 1)]
    for ch, side in by_output:
        fin1(last, ch, side)
    finish_both(last - 1)
    for ch in range(2):
        fin2_last(ch)
        place_start(ch)
    for copy in gather + shared[:3]:
        copy.wait_send()

    for r in range(ROUNDS):
        for ch, side in chains:
            for copy in ring1_of(r, ch, side) + (ring2_of(r, ch, side) if r < last else direct2(ch, side)):
                copy.wait_send()
    for ch in range(2):
        mine[ch].wait()
        place_wait(ch)


def per_device(dlog, dener, energy, mask, owner):
    walkers, width = dlog.shape
    anywhere = pl.BlockSpec(memory_space=pl.ANY)
    dma = pltpu.SemaphoreType.DMA
    both = pl.pallas_call(
        kernel,
        out_shape=jax.ShapeDtypeStruct((2, BLOCK, width), BF16),
        in_specs=[anywhere] * 5,
        out_specs=anywhere,
        scratch_shapes=[
            pltpu.SMEM((16,), jnp.int32),
            pltpu.SMEM((16,), jnp.int32),
            pltpu.VMEM((walkers // 128, 128), F32),
            pltpu.VMEM((8, walkers, BLOCK), BF16),
            pltpu.VMEM((walkers, width), BF16),
            pltpu.VMEM((walkers, width), BF16),
            pltpu.VMEM((walkers, width), BF16),
            pltpu.VMEM((2, 2, 2, walkers, BLOCK), BF16),
            pltpu.VMEM((2 * BLOCK, walkers), BF16),
            pltpu.VMEM((walkers, 128), F32),
            pltpu.VMEM((PAIRS, 2, 2, 2, 4, 64, width), BF16),
            pltpu.VMEM((PAIRS, 2, 2, 6, 64, width), BF16),
            pltpu.VMEM((PAIRS, 2, 2, 2, 4, 16, width), BF16),
            pltpu.VMEM((PAIRS, 2, 2, 6, 16, width), BF16),
            pltpu.VMEM((2, 2, 2, 2, 4, 64, BLOCK), BF16),
            pltpu.VMEM((2, 2, 2, 6, 64, BLOCK), BF16),
            pltpu.VMEM((2, 2, 2, 2, 4, 16, BLOCK), BF16),
            pltpu.VMEM((2, 2, 2, 6, 16, BLOCK), BF16),
            pltpu.VMEM((2, 4, 2, 16, BLOCK), BF16),
            pltpu.VMEM((2, 4, 2, 16, BLOCK), BF16),
            pltpu.VMEM((16, 16, width), F32),
            pltpu.VMEM((16, 16, width), F32),
            pltpu.VMEM((8, 2, 16, width), F32),
            pltpu.VMEM((2, 16, 16, width), BF16),
            pltpu.VMEM((2, 5, 2, 8, BLOCK), F32),
            pltpu.VMEM((4, 2, 8, BLOCK), F32),
            pltpu.VMEM((2, 8, BLOCK), F32),
            dma((6,)), dma((8,)), dma((8,)), dma((2,)), dma((2,)), dma((4,)), dma((4,)), dma((4,)), dma((4,)),
            dma((ROUNDS, 2, 2, 6)), dma((ROUNDS, 2, 2, 6)), dma((ROUNDS, 2, 2, 6)), dma((ROUNDS, 2, 2, 6)),
            dma((8, 2)), dma((8, 2)), dma((16, 2)), dma((16, 2)),
            dma((2, 4)), dma((2, 4)), dma((2, 4)), dma((2, 4)),
        ],
        compiler_params=pltpu.CompilerParams(
            collective_id=0, has_side_effects=True, vmem_limit_bytes=64 * 1000 * 1000
        ),
    )(mask, owner, dlog, dener, energy.reshape(walkers // 128, 128))
    return both[0].astype(F32), both[1].astype(F32)


def solution(mesh):
    return jax.shard_map(
        per_device,
        mesh=mesh,
        in_specs=(P("walk", "pan"), P("walk", "pan"), P("walk"), P(), P()),
        out_specs=(P("walk", "pan"), P("walk", "pan")),
        check_vma=False,
    )
```

```python
import jax
import jax.numpy as jnp
from jax import lax
from jax.experimental import pallas as pl
from jax.experimental.pallas import tpu as pltpu
from jax.sharding import PartitionSpec as P

BLOCK = 256
ROUNDS = 5
PAIRS = 3
MESH = pl.DeviceIdType.MESH
F32 = jnp.float32
BF16 = jnp.bfloat16


def wrap4(v):
    return lax.rem(v, 4)


def kernel(
    mask_in, owner_in, dlog, dener, energy_in, out,
    mask, owner, energy,
    blocks, gown, opar, gpar, right, left_t, spread,
    part, ring1, half, ring2, part_s, ring1_s, half_s, ring2_s,
    near2, cross2, whole_c, whole_h, give, staged, stats, means, pmeans,
    local_sem, ag_send, ag_recv, pt_send, pt_recv, st_send, st_recv, mm_send, mm_recv,
    r1_send, r1_recv, r2_send, r2_recv, z_send, z_recv, f_send, f_recv,
    n2_send, n2_recv, c2_send, c2_recv,
):
    walkers = dlog.shape[0]
    total = walkers * 16
    scale = 1.0 / total
    chunk = 256
    steps = walkers // chunk

    walk = lax.axis_index("walk")
    pan = lax.axis_index("pan")
    px, pz = lax.div(walk, 4), lax.rem(walk, 4)
    py, core = lax.div(pan, 2), lax.rem(pan, 2)
    partner = (walk, py * 2 + (1 - core))

    def at_y(shift):
        return (walk, wrap4(py + shift) * 2 + core)

    def remote(src, dst, send, recv, device):
        return pltpu.make_async_remote_copy(
            src_ref=src, dst_ref=dst, send_sem=send, recv_sem=recv, device_id=device, device_id_type=MESH
        )

    barrier = pltpu.get_barrier_semaphore()

    near = [
        (wrap4(px + 1) * 4 + pz, pan),
        (wrap4(px + 3) * 4 + pz, pan),
        (px * 4 + wrap4(pz + 1), pan),
        (px * 4 + wrap4(pz + 3), pan),
        at_y(1),
        at_y(3),
        partner,
    ]
    for device in near:
        pl.semaphore_signal(barrier, inc=1, device_id=device, device_id_type=MESH)
    small = [
        pltpu.make_async_copy(source, target, local_sem.at[3 + n])
        for n, (source, target) in enumerate(((mask_in, mask), (owner_in, owner), (energy_in, energy)))
    ]
    own = [
        pltpu.make_async_copy(dlog.at[:, pl.ds(b * BLOCK, BLOCK)], blocks.at[b], local_sem.at[b]) for b in range(2)
    ] + [pltpu.make_async_copy(dener, gown, local_sem.at[2])]
    pl.semaphore_wait(barrier, len(near))

    def column(b):
        return dlog.at[:, pl.ds(b * BLOCK, BLOCK)]

    def onward(n, slot, to):
        rows = pl.ds((slot % 2) * (walkers // 2), walkers // 2)
        return remote(
            blocks.at[slot, rows, :], blocks.at[to, rows, :], ag_send.at[n], ag_recv.at[n], at_y(3 if slot % 2 else 1)
        )

    gather = [
        remote(column(0), blocks.at[2], ag_send.at[0], ag_recv.at[0], at_y(1)),
        remote(column(0), blocks.at[3], ag_send.at[1], ag_recv.at[1], at_y(3)),
        remote(column(1), blocks.at[4], ag_send.at[2], ag_recv.at[2], at_y(1)),
        remote(column(1), blocks.at[5], ag_send.at[3], ag_recv.at[3], at_y(3)),
        onward(4, 2, 6),
        onward(5, 3, 6),
        onward(6, 4, 7),
        onward(7, 5, 7),
    ]
    for copy in gather[:2] + own + small:
        copy.start()
    pair = [
        remote(dlog, opar, pt_send.at[0], pt_recv.at[0], partner),
        remote(dener, gpar, pt_send.at[1], pt_recv.at[1], partner),
    ]
    for copy in pair:
        copy.start()

    for copy in own + small:
        copy.wait()
    esum = jnp.sum(energy[...])
    for b in range(2):

        def add(i, carry):
            rows = pl.ds(pl.multiple_of(i * chunk, chunk), chunk)
            o = jnp.sum(blocks[b, rows, :].astype(F32), axis=0, keepdims=True)
            g = jnp.sum(gown[rows, b * BLOCK:(b + 1) * BLOCK].astype(F32), axis=0, keepdims=True)
            return carry[0] + o, carry[1] + g

        zero = jnp.zeros((1, BLOCK), F32)
        o, g = lax.fori_loop(0, steps, add, (zero, zero))
        stats[0, 0, b] = jnp.concatenate([o, g, jnp.full((1, BLOCK), esum, F32), jnp.zeros((5, BLOCK), F32)], axis=0)

    swaps = [
        ((px + 1 - 2 * lax.rem(px, 2)) * 4 + pz, pan),
        ((3 - px) * 4 + pz, pan),
        (px * 4 + pz + 1 - 2 * lax.rem(pz, 2), pan),
        (px * 4 + 3 - pz, pan),
    ]
    for n, device in enumerate(swaps):
        swap = remote(stats.at[0, n], stats.at[1, n], st_send.at[n], st_recv.at[n], device)
        swap.start()
        swap.wait()
        stats[0, n + 1] = stats[0, n] + stats[1, n]
    means[py] = stats[0, 4] * scale
    below = wrap4(py + 3)
    shared = [
        remote(means.at[py], means.at[py], mm_send.at[0], mm_recv.at[0], at_y(1)),
        remote(means.at[py], means.at[py], mm_send.at[1], mm_recv.at[1], at_y(3)),
        remote(means.at[below], means.at[below], mm_send.at[2], mm_recv.at[2], at_y(1)),
        remote(means.at[py], pmeans, mm_send.at[3], mm_recv.at[3], partner),
    ]
    for copy in [shared[0], shared[1], shared[3]] + gather[2:4]:
        copy.start()

    ebar = means[py, 0, 2:3, 0:128]
    for i in range(walkers // 128):
        row = energy[i:i + 1, :] - ebar
        spread[i * 128:(i + 1) * 128, :] = jnp.broadcast_to(row, (128, 128)).T

    def build(o_of, g_of, obar, gbar, m, side, b):
        def step(i, carry):
            rows = pl.ds(pl.multiple_of(i * chunk, chunk), chunk)
            oc = o_of(rows).astype(F32) * m - obar
            e = spread[rows, :]
            hc = jnp.concatenate([e, e], axis=1) * oc + g_of(rows).astype(F32) * m - gbar
            right[0, side, b, rows, :] = oc.astype(BF16)
            right[1, side, b, rows, :] = hc.astype(BF16)
            return carry

        lax.fori_loop(0, steps, step, 0)

    def build_own():
        for b in range(2):
            m = mask[py * 4 + core * 2 + b].astype(F32)
            build(
                lambda rows, b=b: blocks[b, rows, :],
                lambda rows, b=b: gown[rows, b * BLOCK:(b + 1) * BLOCK],
                means[py, b, 0:1, :] * m,
                means[py, b, 1:2, :] * m,
                m,
                0,
                b,
            )

    def build_partner():
        for copy in pair:
            copy.wait()
        shared[3].wait()
        for b in range(2):
            m = mask[py * 4 + (1 - core) * 2 + b].astype(F32)
            build(
                lambda rows, b=b: opar[rows, b * BLOCK:(b + 1) * BLOCK],
                lambda rows, b=b: gpar[rows, b * BLOCK:(b + 1) * BLOCK],
                pmeans[b, 0:1, :] * m,
                pmeans[b, 1:2, :] * m,
                m,
                1,
                b,
            )

    xs = (px, (wrap4(px + 1) * 4 + pz, pan), (wrap4(px + 3) * 4 + pz, pan))
    zs = (pz, (px * 4 + wrap4(pz + 1), pan), (px * 4 + wrap4(pz + 3), pan))

    def ring(buf, got, send, recv, axis):
        me, up, down = axis
        far, nxt, prv = wrap4(me + 2), wrap4(me + 1), wrap4(me + 3)
        return [
            remote(buf.at[0, far], got.at[0], send.at[0], recv.at[0], up),
            remote(buf.at[1, far], got.at[1], send.at[1], recv.at[1], down),
            remote(buf.at[1, nxt], got.at[2], send.at[2], recv.at[2], up),
            remote(buf.at[0, prv], got.at[3], send.at[3], recv.at[3], down),
            remote(buf.at[0, nxt], got.at[4], send.at[4], recv.at[4], up),
            remote(buf.at[1, prv], got.at[5], send.at[5], recv.at[5], down),
        ]

    last = ROUNDS - 1
    chains = [(ch, side) for side in range(2) for ch in range(2)]
    arrivals = ((3, 4), (2, 5))

    def buffers(r):
        return (part, ring1, half, ring2, r) if r < PAIRS else (part_s, ring1_s, half_s, ring2_s, r - PAIRS)

    def ring1_of(r, ch, side):
        buf, got, _, _, n = buffers(r)
        sems = (r, ch, side)
        return ring(buf.at[n, ch, side], got.at[n, ch, side], r1_send.at[sems], r1_recv.at[sems], (xs, zs)[ch])

    def ring2_of(r, ch, side):
        _, _, buf, got, n = buffers(r)
        sems = (r, ch, side)
        return ring(buf.at[n, ch, side], got.at[n, ch, side], r2_send.at[sems], r2_recv.at[sems], (zs, xs)[ch])

    def ring_start(copies):
        for copy in copies[:4]:
            copy.start()

    def ring_mid(copies, buf, got, axis):
        for b, shift in ((0, 1), (1, 3)):
            copies[b].wait_recv()
            k = wrap4(axis[0] + shift)
            buf[b, k] = (buf[b, k].astype(F32) + got[b].astype(F32)).astype(BF16)
            copies[4 + b].start()

    def mid1(r, ch, side):
        buf, got, _, _, n = buffers(r)
        ring_mid(ring1_of(r, ch, side), buf.at[n, ch, side], got.at[n, ch, side], (xs, zs)[ch])

    def mid2(r, ch, side):
        _, _, buf, got, n = buffers(r)
        ring_mid(ring2_of(r, ch, side), buf.at[n, ch, side], got.at[n, ch, side], (zs, xs)[ch])

    def reduced(r, ch, side, b, rows):
        buf, got, _, _, n = buffers(r)
        i, j = arrivals[b]
        own = buf[n, ch, side, b, (px, pz)[ch], rows, :].astype(F32)
        return own + got[n, ch, side, i, rows, :].astype(F32) + got[n, ch, side, j, rows, :].astype(F32)

    def fin1(r, ch, side):
        copies = ring1_of(r, ch, side)
        _, _, buf, _, n = buffers(r)
        for b in range(2):
            for k in arrivals[b]:
                copies[k].wait_recv()
            for k in range(4):
                buf[n, ch, side, b, k] = reduced(r, ch, side, b, slice(16 * k, 16 * k + 16)).astype(BF16)
        if r < last:
            ring_start(ring2_of(r, ch, side))
        else:
            for copy in direct2(ch, side):
                copy.start()

    def direct2(ch, side):
        me = (pz, px)[ch]
        copies = []
        for d in range(1 - side, 4):
            k = wrap4(me + d)
            device = ((px * 4 + k, k * 4 + pz)[ch], py * 2 + (1 - core if side else core))
            copies.append(
                remote(
                    half_s.at[last - PAIRS, ch, side, :, k],
                    (near2, cross2)[side].at[ch, d],
                    (n2_send, c2_send)[side].at[ch, d],
                    (n2_recv, c2_recv)[side].at[ch, d],
                    device,
                )
            )
        return copies

    def fin2_last(ch):
        order = last + PAIRS
        ysrc, bsel = source(order)
        rows = pl.ds(pl.multiple_of((pz, px)[ch] * 16, 16), 16)
        for side in range(2):
            for copy in direct2(ch, side):
                copy.wait_recv()
            for b in range(2):
                value = near2[ch, 1, b].astype(F32) if side == 0 else cross2[ch, 1, b].astype(F32)
                for d in (2, 3):
                    value = value + (near2, cross2)[side][ch, d, b].astype(F32)
                value = value + (reduced(last, ch, 0, b, rows) if side == 0 else cross2[ch, 0, b].astype(F32))
                block = ysrc * 4 + (1 - core if side else core) * 2 + bsel
                whole[ch][block, :, b * BLOCK:(b + 1) * BLOCK] = value * scale

    def fin2(r, ch, side):
        copies = ring2_of(r, ch, side)
        _, _, _, ring, n = buffers(r)
        for b in range(2):
            i, j = arrivals[b]
            copies[i].wait_recv()
            copies[j].wait_recv()
            rows = pl.ds(pl.multiple_of((pz, px)[ch] * 16, 16), 16)
            got = ring[n, ch, side, i].astype(F32) + ring[n, ch, side, j].astype(F32)
            value = (reduced(r, ch, side, b, rows) + got) * scale
            order = 2 * r + b if r < PAIRS else r + PAIRS
            lanes = slice(0, 2 * BLOCK) if r < PAIRS else slice(b * BLOCK, (b + 1) * BLOCK)
            if side == 0:
                whole[ch][block_of(order), :, lanes] = value
            else:
                give[order, ch, :, lanes] = value

    whole = (whole_c, whole_h)
    meets = ((0, 0), (0, 1), (3, 0), (1, 0), (3, 1), (1, 1), (2, 0), (2, 1))

    def source(order):
        return wrap4(py + meets[order][0]), meets[order][1]

    def block_of(order):
        ysrc, bsel = source(order)
        return ysrc * 4 + core * 2 + bsel

    def orders(r):
        return (2 * r, 2 * r + 1) if r < PAIRS else (r + PAIRS,)

    def give_copy(order, ch):
        return remote(
            give.at[order, ch], whole[ch].at[block_of(order)], z_send.at[order, ch], z_recv.at[order, ch], partner
        )

    def gathered(r):
        for k in ((0, 1), (), (2,), ())[r - 1]:
            shared[k].wait_recv()
        if r == 1:
            shared[2].start()
        for b in range(2):
            gather[2 * (r - 1) + b].wait_recv()
            if r <= 2:
                gather[2 * (r + 1) + b].start()

    def load_left(r):
        for b, order in enumerate(orders(r)):
            ysrc, bsel = source(order)
            m = mask[ysrc * 4 + core * 2 + bsel].astype(F32)
            obar = means[ysrc, bsel, 0:1, :] * m

            def turn(i, c):
                rows = pl.ds(pl.multiple_of(i * chunk, chunk), chunk)
                oc = blocks[order, rows, :].astype(F32) * m - obar
                left_t[b * BLOCK:(b + 1) * BLOCK, rows] = oc.T.astype(BF16)
                return c

            lax.fori_loop(0, steps, turn, 0)

    def multiply(r, ch, side):
        for b in range(2):
            if r < PAIRS:
                product = jnp.dot(left_t[...], right[ch, side, b], preferred_element_type=F32).astype(BF16)
                part[r, ch, side, :, :, :, b * BLOCK:(b + 1) * BLOCK] = product.reshape(2, 4, 64, BLOCK)
            else:
                product = jnp.dot(left_t[:BLOCK, :], right[ch, side, b], preferred_element_type=F32).astype(BF16)
                part_s[r - PAIRS, ch, side, b] = product.reshape(4, 64, BLOCK)
        ring_start(ring1_of(r, ch, side))

    def finish(r, ch):
        for side in range(2):
            fin2(r, ch, side)
        for order in orders(r):
            give_copy(order, ch).start()

    build_own()
    load_left(0)
    multiply(0, 0, 0)
    multiply(0, 1, 0)
    build_partner()
    multiply(0, 0, 1)
    multiply(0, 1, 1)
    def every(step, r):
        for ch, side in chains:
            step(r, ch, side)

    def finish_both(r):
        finish(r, 0)
        finish(r, 1)

    between = {
        1: (lambda: every(mid1, 0), None, lambda: every(fin1, 0), None),
        2: (lambda: every(mid2, 1), None, None, None),
        3: (None, None, None, None),
        4: (None, None, None, lambda: every(fin1, 3)),
    }
    after = {
        1: ((every, mid1, 1), (every, mid2, 0), (every, fin1, 1), (finish_both, 0)),
        2: ((finish_both, 1), (every, mid1, 2)),
        3: ((every, fin1, 2), (every, mid1, 3), (every, mid2, 2)),
        4: (),
    }
    for r in range(1, ROUNDS):
        gathered(r)
        load_left(r)
        for (ch, side), also in zip(((0, 0), (0, 1), (1, 0), (1, 1)), between[r]):
            multiply(r, ch, side)
            if also is not None:
                also()
        for call, *arguments in after[r]:
            call(*arguments)

    row_c = pl.multiple_of(px * 64 + pz * 16, 16)
    row_h = pl.multiple_of(pz * 64 + px * 16, 16)

    def place(r, d, ch):
        return remote(
            staged.at[ch, r],
            out.at[ch, pl.ds((row_c, row_h)[ch], 16), :],
            f_send.at[d, ch],
            f_recv.at[d, ch],
            (r, pan),
        )

    mine = [
        pltpu.make_async_copy(
            staged.at[ch, walk], out.at[ch, pl.ds((row_c, row_h)[ch], 16), :], local_sem.at[ch]
        )
        for ch in range(2)
    ]

    def place_start(ch):
        for order in range(last + PAIRS):
            give_copy(order, ch).wait()

        def step(d, carry):
            r = lax.rem(walk + d, 16)
            staged[ch, r] = whole[ch][owner[r]].astype(BF16)
            place(r, d, ch).start()
            return carry

        lax.fori_loop(1, 16, step, 0)
        staged[ch, walk] = whole[ch][owner[walk]].astype(BF16)
        mine[ch].start()

    def place_wait(ch):
        def step(d, carry):
            place(lax.rem(walk + d, 16), d, ch).wait()
            return carry

        lax.fori_loop(1, 16, step, 0)

    by_output = [(0, 0), (0, 1), (1, 0), (1, 1)]
    for ch, side in by_output:
        mid1(last, ch, side)
    every(mid2, last - 1)
    finish_both(last - 2)
    for ch, side in by_output:
        fin1(last, ch, side)
    finish_both(last - 1)
    for ch in range(2):
        fin2_last(ch)
        place_start(ch)
    for copy in gather + shared[:3]:
        copy.wait_send()

    for r in range(ROUNDS):
        for ch, side in chains:
            for copy in ring1_of(r, ch, side) + (ring2_of(r, ch, side) if r < last else direct2(ch, side)):
                copy.wait_send()
    for ch in range(2):
        mine[ch].wait()
        place_wait(ch)


def per_device(dlog, dener, energy, mask, owner):
    walkers, width = dlog.shape
    anywhere = pl.BlockSpec(memory_space=pl.ANY)
    dma = pltpu.SemaphoreType.DMA
    both = pl.pallas_call(
        kernel,
        out_shape=jax.ShapeDtypeStruct((2, BLOCK, width), BF16),
        in_specs=[anywhere] * 5,
        out_specs=anywhere,
        scratch_shapes=[
            pltpu.SMEM((16,), jnp.int32),
            pltpu.SMEM((16,), jnp.int32),
            pltpu.VMEM((walkers // 128, 128), F32),
            pltpu.VMEM((8, walkers, BLOCK), BF16),
            pltpu.VMEM((walkers, width), BF16),
            pltpu.VMEM((walkers, width), BF16),
            pltpu.VMEM((walkers, width), BF16),
            pltpu.VMEM((2, 2, 2, walkers, BLOCK), BF16),
            pltpu.VMEM((2 * BLOCK, walkers), BF16),
            pltpu.VMEM((walkers, 128), F32),
            pltpu.VMEM((PAIRS, 2, 2, 2, 4, 64, width), BF16),
            pltpu.VMEM((PAIRS, 2, 2, 6, 64, width), BF16),
            pltpu.VMEM((PAIRS, 2, 2, 2, 4, 16, width), BF16),
            pltpu.VMEM((PAIRS, 2, 2, 6, 16, width), BF16),
            pltpu.VMEM((2, 2, 2, 2, 4, 64, BLOCK), BF16),
            pltpu.VMEM((2, 2, 2, 6, 64, BLOCK), BF16),
            pltpu.VMEM((2, 2, 2, 2, 4, 16, BLOCK), BF16),
            pltpu.VMEM((2, 2, 2, 6, 16, BLOCK), BF16),
            pltpu.VMEM((2, 4, 2, 16, BLOCK), BF16),
            pltpu.VMEM((2, 4, 2, 16, BLOCK), BF16),
            pltpu.VMEM((16, 16, width), F32),
            pltpu.VMEM((16, 16, width), F32),
            pltpu.VMEM((8, 2, 16, width), F32),
            pltpu.VMEM((2, 16, 16, width), BF16),
            pltpu.VMEM((2, 5, 2, 8, BLOCK), F32),
            pltpu.VMEM((4, 2, 8, BLOCK), F32),
            pltpu.VMEM((2, 8, BLOCK), F32),
            dma((6,)), dma((8,)), dma((8,)), dma((2,)), dma((2,)), dma((4,)), dma((4,)), dma((4,)), dma((4,)),
            dma((ROUNDS, 2, 2, 6)), dma((ROUNDS, 2, 2, 6)), dma((ROUNDS, 2, 2, 6)), dma((ROUNDS, 2, 2, 6)),
            dma((8, 2)), dma((8, 2)), dma((16, 2)), dma((16, 2)),
            dma((2, 4)), dma((2, 4)), dma((2, 4)), dma((2, 4)),
        ],
        compiler_params=pltpu.CompilerParams(
            collective_id=0, has_side_effects=True, vmem_limit_bytes=64 * 1000 * 1000
        ),
    )(mask, owner, dlog, dener, energy.reshape(walkers // 128, 128))
    return both[0].astype(F32), both[1].astype(F32)


def solution(mesh):
    return jax.shard_map(
        per_device,
        mesh=mesh,
        in_specs=(P("walk", "pan"), P("walk", "pan"), P("walk"), P(), P()),
        out_specs=(P("walk", "pan"), P("walk", "pan")),
        check_vma=False,
    )
```
